256 devices in a mesh: blk: 16 (over x_lo, y, core), mod: 16 (over x_hi, z).
Axes of the slice: x: 4 (x_hi: 2, x_lo: 2; x = x_hi * 2 + x_lo), y: 4, z: 8, core: 2. Of those that a mesh axis runs over, the one named last changes fastest.
Arguments:
- act: bfloat16 [16, 32, 16384], P('mod', None, 'blk'), may hold values from -6 to 6
- grad: bfloat16 [16, 64, 16384], P('mod', None, 'blk'), may hold values from -40 to 40
- train: bfloat16 [16, 32768, 2048], P('mod', 'blk'), may hold values from -24 to 24
- pre_out: float32 [16, 64, 64], P('mod'), may hold values from -0.75 to 0.75
- pre_in: float32 [16, 32, 32], P('mod'), may hold values from -1 to 1
- doc_ids: int32 [16384, 1], P('blk'), may hold values from 0 to 511; in each aligned block of 1024 rows (0 to 1023, 1024 to 2047, ...) at most 4 rows name the same one
- owners: int32 [512], replicated, may hold values from 0 to 511, each once
Outputs:
- scores: float32 [16, 512, 32768], P('mod', None, 'blk')
The draws below stay inside these ranges and needn't reach their ends.
Inputs may be any that keep to these rules, and one draw needn't show every extreme that they name: `doc_ids`: among the 1024 tokens of one index of blk no document has more than 4 tokens, and some document has exactly 4 in some such block; every document has at least one token. `owners`: A permutation of the 512 documents.
All inputs are finite; a program needn't handle non-finite values.
Results may differ from the reference program's by a relative error of at most 0.0029.
Values may be sent and summed in bfloat16 or wider, within the bound.
No kernel may reach another device: no remote copies, remote signals or barrier semaphores. Data moves between devices by JAX's collectives and lax.ppermute only.
A program may use at most 64 MiB of HBM per device.

```python
import math
import jax
import jax.numpy as jnp
import numpy as np
from jax import lax

A = 32
G = 64
MOST = 4
TOK_DEV = 1024
MODULES = 16
DOCS = 512
QTOK = 16384
TRAIN = 32768
N_BLK = 16


def draw_grad(key, part):
    token_key = jax.random.fold_in(jax.random.fold_in(key, 7), 1)
    value_key = jax.random.fold_in(jax.random.fold_in(key, 7), 2)
    level = jnp.arange(MODULES, dtype=jnp.float32) / max(MODULES - 1, 1)
    token_scale = jnp.exp(jax.random.uniform(token_key, (QTOK,), jnp.float32, jnp.log(0.3), jnp.log(3.0)))
    values = jnp.clip(jax.random.normal(value_key, (MODULES, G, QTOK), jnp.float32), -4.0, 4.0)
    module_scale = 3.0 ** level
    return (values * module_scale[:, None, None] * token_scale[None, None, :]).astype(jnp.bfloat16)


def block_scale(stream_key, extent, pieces, least, high):
    level = 1.0
    for axis_at, parts in pieces:
        steps = jax.random.uniform(jax.random.fold_in(jax.random.fold_in(stream_key, 6), axis_at), (parts,), jnp.float32, least / len(pieces), high / len(pieces))
        level = level * jnp.repeat(jnp.exp(steps), extent[axis_at] // parts).reshape((-1,) + (1,) * (len(extent) - 1 - axis_at))
    return level


def deal_out(rng, own, number, rows, number_of, top, bound, skew):
    sequence = jax.random.permutation(rng, number_of)
    crowded, usual = portions_of(number_of, rows * top, bound, skew, True), portions_of(number_of, rows * top, bound, skew, False)
    places = jnp.arange(number_of)

    def named(lengths, turn):
        used = int((lengths > 0).sum())
        fixed = max(1, used // 4)
        moved = fixed + (places - fixed + turn * (used - fixed)) % max(1, number_of - fixed)
        return jnp.zeros((number_of,), jnp.int32).at[sequence[jnp.where(places < fixed, places, moved)]].set(jnp.asarray(lengths, jnp.int32))

    lengths = jnp.where(number % 4 == 0, named(crowded, number // 4), named(usual, number - number // 4 - 1))
    mixed = jax.random.permutation(jax.random.fold_in(own, 3), number_of)
    source_of, taker = mixed[0:number_of // 2 * 2:2], mixed[1:number_of // 2 * 2:2]
    room = jnp.minimum(lengths[source_of] - 1, bound - lengths[taker]) // 2
    room = jnp.where((source_of == sequence[0]) | (taker == sequence[0]) | (lengths[taker] == 0), 0, jnp.maximum(room, 0))
    moved = jax.random.randint(jax.random.fold_in(own, 4), (number_of // 2,), 0, 1 << 20) % (room + 1)
    lengths = lengths.at[source_of].add(-moved).at[taker].add(moved)
    labels = jnp.searchsorted(jnp.cumsum(lengths), jnp.arange(rows * top), side="right").astype(jnp.int32)
    table = labels.reshape(top, rows).T
    table = table[jax.random.permutation(jax.random.fold_in(own, 1), rows)]
    turn = jax.random.randint(jax.random.fold_in(own, 2), (rows, 1), 0, top)
    return jnp.take_along_axis(table, (jnp.arange(top)[None, :] + turn) % top, axis=1)


def portions_of(count, total, most, skew, full):
    weights = [(1 << 20) // math.isqrt(standing ** skew) + 1 for standing in range(1, count + 1)]
    largest = most if full else min(most, max(-(-total // count), total * weights[0] // sum(weights)))
    least = 1 if total - largest >= count - 1 else 0
    given, spare = [largest] + [least] * (count - 1), total - largest - least * (count - 1)
    while spare > 0:
        free = [i for i in range(1, count) if given[i] < largest] or [i for i in range(1, count) if given[i] < most]
        pool, left = sum([weights[i] for i in free]), spare
        for i in free:
            addition = min(most - given[i], max(1, left * weights[i] // pool), spare)
            given[i] = given[i] + addition
            spare = spare - addition
    return np.array(given)


def noise(key, extent, spread, most, pieces=(), kind=jnp.bfloat16):
    result = jax.random.normal(key, extent, jnp.float32) * spread
    if len(pieces) > 0:
        result = block_scale(key, extent, pieces, -0.22, 0.18) * result
    return jnp.clip(result, min=-most, max=most).astype(kind)


def setup_inputs(seed: int = 0) -> dict:
    seeds = jax.random.split(jax.random.key(seed), 8)
    act = noise(seeds[0], (MODULES, A, QTOK), 1.0, 6.0, ((0, 16), (2, 16)))
    grad = draw_grad(jax.random.fold_in(seeds[7], 71), 0)
    train = noise(seeds[2], (MODULES, TRAIN, G * A), 4.0, 24.0, ((0, 16), (1, 16)))
    pre_out = noise(seeds[3], (MODULES, G, G), G ** -0.5, 0.75, ((0, 16),), jnp.float32)
    pre_in = noise(seeds[4], (MODULES, A, A), A ** -0.5, 1.0, ((0, 16),), jnp.float32)
    doc_ids_keys = jax.random.split(jax.random.fold_in(seeds[5], 1), QTOK // TOK_DEV)
    doc_ids_turns = jax.random.permutation(jax.random.fold_in(seeds[5], 3), QTOK // TOK_DEV)
    doc_ids = jax.vmap(lambda own, number: deal_out(jax.random.fold_in(seeds[5], 2), own, number, TOK_DEV, DOCS, 1, MOST, 2))(doc_ids_keys, doc_ids_turns).reshape((QTOK, 1))
    owners = jax.random.permutation(seeds[6], DOCS).astype(jnp.int32)
    return dict(act=act, grad=grad, train=train, pre_out=pre_out, pre_in=pre_in, doc_ids=doc_ids, owners=owners)


def reference(act, grad, train, pre_out, pre_in, doc_ids, owners):
    doc_index = doc_ids[:, 0]
    onehot = (doc_index[:, None] == jnp.arange(DOCS, dtype=jnp.int32)[None, :]).astype(jnp.float32)

    def per_module(module):
        act_rows = act[module].astype(jnp.float32)
        grad_rows = grad[module].astype(jnp.float32)

        def step(total, block):
            act_block = lax.dynamic_slice_in_dim(act_rows, block * TOK_DEV, TOK_DEV, 1)
            grad_block = lax.dynamic_slice_in_dim(grad_rows, block * TOK_DEV, TOK_DEV, 1)
            hot_block = lax.dynamic_slice_in_dim(onehot, block * TOK_DEV, TOK_DEV, 0)
            outer = (grad_block[:, None, :] * act_block[None, :, :]).reshape(G * A, TOK_DEV)
            return (total + jnp.dot(outer, hot_block, precision=lax.Precision.HIGHEST), None)
        total, _ = lax.scan(step, jnp.zeros((G * A, DOCS), jnp.float32), jnp.arange(N_BLK, dtype=jnp.int32))
        doc_grad = total.T.reshape(DOCS, G, A)
        left = jnp.einsum('hg,dga->dha', pre_out[module], doc_grad, precision=lax.Precision.HIGHEST)
        return jnp.einsum('dha,ab->dhb', left, pre_in[module], precision=lax.Precision.HIGHEST)
    cond = lax.map(per_module, jnp.arange(MODULES, dtype=jnp.int32))
    squares = lax.optimization_barrier(jnp.sum(cond * cond, axis=(0, 2, 3)))
    inv_norm = 1.0 / jnp.sqrt(squares + 1e-06)
    ordered = cond[:, owners] * inv_norm[owners][None, :, None, None]
    doc_b = ordered.reshape(MODULES, DOCS, G * A).astype(jnp.bfloat16)

    def score_module(module):
        return lax.dot_general(doc_b[module], train[module], (((1,), (1,)), ((), ())), preferred_element_type=jnp.float32)
    return lax.map(score_module, jnp.arange(MODULES, dtype=jnp.int32))
```

```python
import functools

import jax
import jax.numpy as jnp
from jax import lax
from jax.experimental import pallas as pl
from jax.experimental.pallas import tpu as pltpu
from jax.sharding import Mesh, PartitionSpec as P

A = 32
G = 64
W = A + G
MOST = 4
BLK = 16
OWN = 32
DOCS = 512
TOK = 1024
LANES = OWN * MOST
F = G * A
BF = jnp.bfloat16
F32 = jnp.float32
NT = (((1,), (1,)), ((), ()))
BLK_AXES = ("xl", "y", "core")
MOD_AXES = ("xh", "z")
VM = pl.BlockSpec(memory_space=pltpu.VMEM)


def iota(shape, axis):
    return lax.broadcasted_iota(jnp.int32, shape, axis)


def slot_kernel(act_ref, grad_ref, ids_ref, own_ref, send_ref):
    ids = ids_ref[...]
    ids_col = jnp.transpose(jnp.broadcast_to(ids, (8, TOK)))[:, :1]
    own_col = jnp.transpose(jnp.broadcast_to(own_ref[...], (8, DOCS)))[:, :1]
    place = jnp.sum(jnp.where(own_col == ids, iota((DOCS, TOK), 0), 0), axis=0, keepdims=True)
    step = 128
    ranks = []
    for j in range(TOK // step):
        mine = ids[:, j * step : (j + 1) * step]
        there = ids_col[j * step : (j + 1) * step]
        same = (there == mine) & (iota((step, step), 0) < iota((step, step), 1))
        count = jnp.sum(same.astype(jnp.int32), axis=0, keepdims=True)
        if j:
            count += jnp.sum((ids_col[: j * step] == mine).astype(jnp.int32), axis=0, keepdims=True)
        ranks.append(count)
    slot = place * MOST + jnp.concatenate(ranks, axis=1)
    group = slot // 256
    inner = slot % 256
    hot = (iota((256, TOK), 0) == inner).astype(F32).astype(BF)
    rows = jnp.concatenate([act_ref[0], grad_ref[0]], axis=0)
    zero = jnp.zeros_like(rows)
    for o in range(BLK // 2):
        part = jnp.where(group == o, rows, zero)
        got = lax.dot_general(part, hot, NT, preferred_element_type=F32).astype(BF)
        send_ref[2 * o] = got[:, :LANES]
        send_ref[2 * o + 1] = got[:, LANES:]


def split(x):
    hi = x.astype(BF)
    return hi, (x - hi.astype(F32)).astype(BF)


def dot(a, b):
    return jnp.dot(a, b, preferred_element_type=F32)


def cond_kernel(recv_ref, po_ref, pi_ref, cond_ref, square_ref):
    doc = jnp.zeros((G, OWN * A), F32)
    mask = (iota((OWN * A, LANES), 0) // A) == (iota((OWN * A, LANES), 1) // MOST)
    wide = jnp.concatenate([mask, mask], axis=1)
    for s in range(0, BLK, 2):
        act = jnp.concatenate([recv_ref[s, :A], recv_ref[s + 1, :A]], axis=1)
        grad = jnp.concatenate([recv_ref[s, A:], recv_ref[s + 1, A:]], axis=1)
        spread = jnp.concatenate([act] * OWN, axis=0)
        spread = jnp.where(wide, spread, jnp.zeros_like(spread))
        doc += lax.dot_general(grad, spread, NT, preferred_element_type=F32)
    po_hi, po_lo = split(po_ref[0])
    d_hi, d_lo = split(doc)
    left = dot(
        jnp.concatenate([po_hi, po_hi, po_lo, po_lo], axis=1),
        jnp.concatenate([d_hi, d_lo, d_hi, d_lo], axis=0),
    )
    pick = (iota((A, 256), 0) == iota((A, 256), 1) % A).astype(F32).astype(BF)
    diag = (iota((256, 256), 0) // A) == (iota((256, 256), 1) // A)

    def block_diagonal(part):
        row = dot(part, pick)
        full = jnp.concatenate([row] * 8, axis=0)
        return jnp.where(diag, full, 0.0).astype(BF)

    pi_hi, pi_lo = split(pi_ref[0])
    pi_hi, pi_lo = block_diagonal(pi_hi), block_diagonal(pi_lo)
    l_hi, l_lo = split(left)
    outs = []
    for q in range(OWN * A // 256):
        cols = slice(q * 256, (q + 1) * 256)
        outs.append(dot(l_hi[:, cols], pi_hi) + dot(l_lo[:, cols], pi_hi) + dot(l_hi[:, cols], pi_lo))
    cond = jnp.concatenate(outs, axis=1)
    cond = jnp.transpose(cond.reshape(G, OWN, A), (1, 0, 2)).reshape(OWN, F)
    cond_ref[...] = cond
    square = jnp.sum(cond * cond, axis=1, keepdims=True)
    row = jnp.transpose(jnp.broadcast_to(square, (OWN, 128)))[:8]
    row = jnp.concatenate([row, jnp.zeros((8, 128 - OWN), F32)], axis=1)
    for m in range(BLK):
        square_ref[m] = row


def scale_kernel(cond_ref, squares_ref, doc_ref):
    total = jnp.sum(squares_ref[...], axis=0)
    inverse = 1.0 / jnp.sqrt(total + 1e-6)
    inverse = jnp.transpose(jnp.broadcast_to(inverse[:1], (8, 128)))[:OWN, :1]
    doc_ref[...] = (cond_ref[...] * inverse).astype(BF)


def score_kernel(count, from_ref, *refs):
    blocks, train_ref, out_ref, docs_ref = refs[:count], refs[count], refs[count + 1], refs[count + 2]

    @pl.when(pl.program_id(0) == 0)
    def _():
        for i in range(count):
            at = pl.multiple_of(from_ref[i] * OWN, OWN)
            docs_ref[pl.ds(at, OWN), :] = blocks[i][...]

    out_ref[0] = lax.dot_general(docs_ref[...], train_ref[0], NT, preferred_element_type=F32)


def swap(x, axis):
    return lax.ppermute(x, axis, [(0, 1), (1, 0)])


def turn(x, by):
    return lax.ppermute(x, "y", [(i, (i + by) % 4) for i in range(4)])


def gather_docs(doc):
    x, y, c = (lax.axis_index(a) for a in BLK_AXES)

    def source(dx, dy, dc):
        return ((x ^ dx) * 4 + (y + dy) % 4) * 2 + (c ^ dc)

    half = OWN // 2
    got = {(0, 0): doc}
    got[1, 0] = swap(doc, "xl")
    got[0, 3] = turn(doc, 1)
    got[0, 1] = turn(doc, -1)
    got[1, 3] = swap(got[0, 3], "xl")
    got[0, 2] = turn(got[0, 3], 1)
    got[1, 1] = turn(got[1, 0], -1)
    last = [swap(got[0, 2][:half], "xl"), turn(got[1, 1][half:], -1)]
    mates = {k: swap(v, "core") for k, v in got.items()}
    got[1, 2] = jnp.concatenate(last, axis=0)
    mates[1, 2] = jnp.concatenate([swap(v, "core") for v in last], axis=0)
    blocks = [*got.values(), *mates.values()]
    places = [source(*k, 0) for k in got] + [source(*k, 1) for k in mates]
    return blocks, jnp.stack(places).astype(jnp.int32)


def body(act, grad, train, pre_out, pre_in, doc_ids, owners):
    send = pl.pallas_call(
        slot_kernel,
        out_shape=jax.ShapeDtypeStruct((BLK, W, LANES), BF),
        in_specs=[VM] * 4,
        out_specs=VM,
        name="slots",
    )(act, grad, doc_ids.reshape(1, TOK), owners.reshape(1, DOCS))
    received = lax.all_to_all(send, BLK_AXES, split_axis=0, concat_axis=0, tiled=True)
    cond, squares = pl.pallas_call(
        cond_kernel,
        out_shape=(
            jax.ShapeDtypeStruct((OWN, F), F32),
            jax.ShapeDtypeStruct((BLK, 8, 128), F32),
        ),
        in_specs=[VM] * 3,
        out_specs=(VM, VM),
        name="condition",
    )(received, pre_out, pre_in)
    squares = lax.all_to_all(squares, MOD_AXES, split_axis=0, concat_axis=0, tiled=True)
    doc = pl.pallas_call(
        scale_kernel,
        out_shape=jax.ShapeDtypeStruct((OWN, F), BF),
        in_specs=[VM] * 2,
        out_specs=VM,
        name="scale",
    )(cond, squares)
    blocks, places = gather_docs(doc)
    tile = 256
    rows = train.shape[1]
    return pl.pallas_call(
        functools.partial(score_kernel, len(blocks)),
        out_shape=jax.ShapeDtypeStruct((1, DOCS, rows), F32),
        grid_spec=pltpu.PrefetchScalarGridSpec(
            num_scalar_prefetch=1,
            grid=(rows // tile,),
            in_specs=[VM] * len(blocks) + [pl.BlockSpec((1, tile, F), lambda i, s: (0, i, 0))],
            out_specs=pl.BlockSpec((1, DOCS, tile), lambda i, s: (0, 0, i)),
            scratch_shapes=[pltpu.VMEM((DOCS, F), BF)],
        ),
        name="scores",
    )(places, *blocks, train)


def solution(mesh):
    fine = Mesh(mesh.devices.reshape(2, 4, 2, 2, 8), (*BLK_AXES, *MOD_AXES))
    return jax.shard_map(
        body,
        mesh=fine,
        in_specs=(
            P(MOD_AXES, None, BLK_AXES),
            P(MOD_AXES, None, BLK_AXES),
            P(MOD_AXES, BLK_AXES, None),
            P(MOD_AXES, None, None),
            P(MOD_AXES, None, None),
            P(BLK_AXES, None),
            P(),
        ),
        out_specs=P(MOD_AXES, None, BLK_AXES),
        check_vma=False,
    )
```

```python
import functools

import jax
import jax.numpy as jnp
from jax import lax
from jax.experimental import pallas as pl
from jax.experimental.pallas import tpu as pltpu
from jax.sharding import Mesh, PartitionSpec as P

A = 32
G = 64
W = A + G
MOST = 4
BLK = 16
OWN = 32
DOCS = 512
TOK = 1024
LANES = OWN * MOST
F = G * A
BF = jnp.bfloat16
F32 = jnp.float32
NT = (((1,), (1,)), ((), ()))
BLK_AXES = ("xl", "y", "core")
MOD_AXES = ("xh", "z")
VM = pl.BlockSpec(memory_space=pltpu.VMEM)


def room(mib):
    return pltpu.CompilerParams(vmem_limit_bytes=mib << 20)


def iota(shape, axis):
    return lax.broadcasted_iota(jnp.int32, shape, axis)


def slot_kernel(act_hbm, grad_hbm, ids_hbm, own_hbm, po_hbm, pi_hbm, train_hbm, send_ref, po_ref, pi_ref, train_ref,
                act_ref, grad_ref, ids_ref, own_ref, sem):
    sources = (ids_hbm, own_hbm, act_hbm, grad_hbm, po_hbm, pi_hbm, train_hbm)
    targets = (ids_ref, own_ref, act_ref, grad_ref, po_ref, pi_ref, train_ref)
    copies = [pltpu.make_async_copy(a, b, sem.at[i]) for i, (a, b) in enumerate(zip(sources, targets))]
    for copy in copies:
        copy.start()
    copies[0].wait()
    copies[1].wait()
    ids = ids_ref[...]
    ids_col = jnp.transpose(jnp.broadcast_to(ids, (8, TOK)))[:, :1]
    own_col = jnp.transpose(jnp.broadcast_to(own_ref[...], (8, DOCS)))[:, :1]
    place = jnp.sum(jnp.where(own_col == ids, iota((DOCS, TOK), 0), 0), axis=0, keepdims=True)
    step = 128
    ranks = []
    for j in range(TOK // step):
        mine = ids[:, j * step : (j + 1) * step]
        there = ids_col[j * step : (j + 1) * step]
        same = (there == mine) & (iota((step, step), 0) < iota((step, step), 1))
        count = jnp.sum(same.astype(jnp.int32), axis=0, keepdims=True)
        if j:
            count += jnp.sum((ids_col[: j * step] == mine).astype(jnp.int32), axis=0, keepdims=True)
        ranks.append(count)
    slot = place * MOST + jnp.concatenate(ranks, axis=1)
    group = slot // 256
    inner = slot % 256
    hot = (iota((256, TOK), 0) == inner).astype(F32).astype(BF)
    copies[2].wait()
    copies[3].wait()
    rows = jnp.concatenate([act_ref[0], grad_ref[0]], axis=0)
    zero = jnp.zeros_like(rows)
    for o in range(BLK // 2):
        part = jnp.where(group == o, rows, zero)
        got = lax.dot_general(part, hot, NT, preferred_element_type=F32).astype(BF)
        send_ref[2 * o] = got[:, :LANES]
        send_ref[2 * o + 1] = got[:, LANES:]
    for copy in copies[4:]:
        copy.wait()


def split(x):
    hi = x.astype(BF)
    return hi, (x - hi.astype(F32)).astype(BF)


def dot(a, b):
    return jnp.dot(a, b, preferred_element_type=F32)


def cond_kernel(recv_ref, po_ref, pi_ref, cond_ref, square_ref):
    doc = jnp.zeros((G, OWN * A), F32)
    mask = (iota((OWN * A, LANES), 0) // A) == (iota((OWN * A, LANES), 1) // MOST)
    wide = jnp.concatenate([mask, mask], axis=1)
    for s in range(0, BLK, 2):
        act = jnp.concatenate([recv_ref[s, :A], recv_ref[s + 1, :A]], axis=1)
        grad = jnp.concatenate([recv_ref[s, A:], recv_ref[s + 1, A:]], axis=1)
        spread = jnp.concatenate([act] * OWN, axis=0)
        spread = jnp.where(wide, spread, jnp.zeros_like(spread))
        doc += lax.dot_general(grad, spread, NT, preferred_element_type=F32)
    po_hi, po_lo = split(po_ref[0])
    d_hi, d_lo = split(doc)
    left = dot(
        jnp.concatenate([po_hi, po_hi, po_lo, po_lo], axis=1),
        jnp.concatenate([d_hi, d_lo, d_hi, d_lo], axis=0),
    )
    pick = (iota((A, 256), 0) == iota((A, 256), 1) % A).astype(F32).astype(BF)
    diag = (iota((256, 256), 0) // A) == (iota((256, 256), 1) // A)

    def block_diagonal(part):
        row = dot(part, pick)
        full = jnp.concatenate([row] * 8, axis=0)
        return jnp.where(diag, full, 0.0).astype(BF)

    pi_hi, pi_lo = split(pi_ref[0])
    pi_hi, pi_lo = block_diagonal(pi_hi), block_diagonal(pi_lo)
    l_hi, l_lo = split(left)
    outs = []
    for q in range(OWN * A // 256):
        cols = slice(q * 256, (q + 1) * 256)
        outs.append(dot(l_hi[:, cols], pi_hi) + dot(l_lo[:, cols], pi_hi) + dot(l_hi[:, cols], pi_lo))
    cond = jnp.concatenate(outs, axis=1)
    cond = jnp.transpose(cond.reshape(G, OWN, A), (1, 0, 2)).reshape(OWN, F)
    cond_ref[...] = cond
    square = jnp.sum(cond * cond, axis=1, keepdims=True)
    row = jnp.transpose(jnp.broadcast_to(square, (OWN, 128)))[:8]
    row = jnp.concatenate([row, jnp.zeros((8, 128 - OWN), F32)], axis=1)
    for m in range(BLK):
        square_ref[m] = row


def scale_kernel(cond_ref, squares_ref, doc_ref):
    total = jnp.sum(squares_ref[...], axis=0)
    inverse = 1.0 / jnp.sqrt(total + 1e-6)
    inverse = jnp.transpose(jnp.broadcast_to(inverse[:1], (8, 128)))[:OWN, :1]
    doc_ref[...] = (cond_ref[...] * inverse).astype(BF)


def score_kernel(places, *refs):
    count = len(places)
    blocks, train_ref, out_hbm, buffer, sem = refs[:count], refs[count], *refs[-3:]
    x, y, c = (lax.axis_index(a) for a in BLK_AXES)
    docs = jnp.concatenate([b[...] for b in blocks], axis=0)
    tile = 512
    copies = []
    for i in range(buffer.shape[1] // tile):
        cols = pl.ds(i * tile, tile)
        buffer[:, cols] = lax.dot_general(docs, train_ref[0, cols, :], NT, preferred_element_type=F32)
        for j, (dx, dy, dc) in enumerate(places):
            at = (((x ^ dx) * 4 + (y + dy) % 4) * 2 + (c ^ dc)) * OWN
            copy = pltpu.make_async_copy(
                buffer.at[pl.ds(j * OWN, OWN), cols],
                out_hbm.at[0, pl.ds(pl.multiple_of(at, OWN), OWN), cols],
                sem.at[i, j],
            )
            copy.start()
            copies.append(copy)
    for copy in copies:
        copy.wait()


def swap(x, axis):
    return lax.ppermute(x, axis, [(0, 1), (1, 0)])


def turn(x, by):
    return lax.ppermute(x, "y", [(i, (i + by) % 4) for i in range(4)])


def score(name, places, blocks, train, out=None):
    rows = train.shape[1]
    hbm = pl.BlockSpec(memory_space=pltpu.HBM)
    more = () if out is None else (out,)
    return pl.pallas_call(
        functools.partial(score_kernel, places),
        out_shape=pltpu.HBM((1, DOCS, rows), F32),
        in_specs=[VM] * (len(blocks) + 1) + [hbm] * len(more),
        out_specs=hbm,
        scratch_shapes=[
            pltpu.VMEM((len(blocks) * OWN, rows), F32),
            pltpu.SemaphoreType.DMA((rows // 512, len(blocks))),
        ],
        input_output_aliases={len(blocks) + 1: 0} if more else {},
        name=name,
        compiler_params=room(8),
    )(*blocks, train, *more)


def pair(block):
    return [block, swap(block, "core")]


def label(*offsets):
    return [(dx, dy, dc) for dx, dy in offsets for dc in (0, 1)]


def body(act, grad, train, pre_out, pre_in, doc_ids, owners):
    hbm = pl.BlockSpec(memory_space=pltpu.HBM)
    ids, own = doc_ids.reshape(1, TOK), owners.reshape(1, DOCS)
    kept = (pre_out, pre_in, train)
    loaded = (act, grad, ids, own)
    send, pre_out, pre_in, train = pl.pallas_call(
        slot_kernel,
        out_shape=(
            jax.ShapeDtypeStruct((BLK, W, LANES), BF),
            *(pltpu.VMEM(v.shape, v.dtype) for v in kept),
        ),
        in_specs=[hbm] * 7,
        out_specs=[VM] * 4,
        scratch_shapes=[
            *(pltpu.VMEM(v.shape, v.dtype) for v in loaded),
            pltpu.SemaphoreType.DMA((7,)),
        ],
        name="slots",
        compiler_params=room(24),
    )(*(pltpu.with_memory_space_constraint(v, pltpu.HBM) for v in (*loaded, *kept)))
    received = lax.all_to_all(send, BLK_AXES, split_axis=0, concat_axis=0, tiled=True)
    cond, squares = pl.pallas_call(
        cond_kernel,
        out_shape=(
            jax.ShapeDtypeStruct((OWN, F), F32),
            jax.ShapeDtypeStruct((BLK, 8, 128), F32),
        ),
        in_specs=[VM] * 3,
        out_specs=(VM, VM),
        name="condition",
        compiler_params=room(16),
    )(received, pre_out, pre_in)
    squares = lax.all_to_all(squares, MOD_AXES, split_axis=0, concat_axis=0, tiled=True)
    doc = pl.pallas_call(
        scale_kernel,
        out_shape=jax.ShapeDtypeStruct((OWN, F), BF),
        in_specs=[VM] * 2,
        out_specs=VM,
        name="scale",
        compiler_params=room(2),
    )(cond, squares)
    side, above, below, over = swap(doc, "xl"), turn(doc, 1), turn(doc, -1), turn(doc, 2)
    near = pair(doc) + pair(side) + pair(above) + pair(below)
    side_above, side_below, side_over = swap(above, "xl"), turn(side, -1), swap(over, "xl")
    out = score("near", label((0, 0), (1, 0), (0, 3), (0, 1)), near, train)
    far = lax.optimization_barrier((over, side_above, side_below, side_over, out))
    over, side_above, side_below, side_over, out = far
    far = pair(over) + pair(side_above) + pair(side_below) + pair(side_over)
    return score("far", label((0, 2), (1, 3), (1, 1), (1, 2)), far, train, out)


def solution(mesh):
    fine = Mesh(mesh.devices.reshape(2, 4, 2, 2, 8), (*BLK_AXES, *MOD_AXES))
    return jax.shard_map(
        body,
        mesh=fine,
        in_specs=(
            P(MOD_AXES, None, BLK_AXES),
            P(MOD_AXES, None, BLK_AXES),
            P(MOD_AXES, BLK_AXES, None),
            P(MOD_AXES, None, None),
            P(MOD_AXES, None, None),
            P(BLK_AXES, None),
            P(),
        ),
        out_specs=P(MOD_AXES, None, BLK_AXES),
        check_vma=False,
    )
```

```python
import functools

import jax
import jax.numpy as jnp
from jax import lax
from jax.experimental import pallas as pl
from jax.experimental.pallas import tpu as pltpu
from jax.sharding import Mesh, PartitionSpec as P

A = 32
G = 64
W = A + G
MOST = 4
BLK = 16
OWN = 32
DOCS = 512
TOK = 1024
LANES = OWN * MOST
F = G * A
TILE = 512
BF = jnp.bfloat16
F32 = jnp.float32
NT = (((1,), (1,)), ((), ()))
BLK_AXES = ("xl", "y", "core")
MOD_AXES = ("xh", "z")
VM = pl.BlockSpec(memory_space=pltpu.VMEM)


def room(mib):
    return pltpu.CompilerParams(vmem_limit_bytes=mib << 20)


def iota(shape, axis):
    return lax.broadcasted_iota(jnp.int32, shape, axis)


def slot_kernel(act_hbm, grad_hbm, ids_hbm, own_hbm, po_hbm, pi_hbm, train_hbm, send_ref, po_ref, pi_ref, train_ref,
                act_ref, grad_ref, ids_ref, own_ref, sem):
    sources = (ids_hbm, own_hbm, act_hbm, grad_hbm, po_hbm, pi_hbm, train_hbm)
    targets = (ids_ref, own_ref, act_ref, grad_ref, po_ref, pi_ref, train_ref)
    copies = [pltpu.make_async_copy(a, b, sem.at[i]) for i, (a, b) in enumerate(zip(sources, targets))]
    for copy in copies:
        copy.start()
    copies[0].wait()
    copies[1].wait()
    ids = ids_ref[...]
    ids_col = jnp.transpose(jnp.broadcast_to(ids, (8, TOK)))[:, :1]
    own_col = jnp.transpose(jnp.broadcast_to(own_ref[...], (8, DOCS)))[:, :1]
    place = jnp.sum(jnp.where(own_col == ids, iota((DOCS, TOK), 0), 0), axis=0, keepdims=True)
    step = 128
    ranks = []
    for j in range(TOK // step):
        mine = ids[:, j * step : (j + 1) * step]
        there = ids_col[j * step : (j + 1) * step]
        same = (there == mine) & (iota((step, step), 0) < iota((step, step), 1))
        count = jnp.sum(same.astype(jnp.int32), axis=0, keepdims=True)
        if j:
            count += jnp.sum((ids_col[: j * step] == mine).astype(jnp.int32), axis=0, keepdims=True)
        ranks.append(count)
    slot = place * MOST + jnp.concatenate(ranks, axis=1)
    group = slot // 256
    inner = slot % 256
    hot = (iota((256, TOK), 0) == inner).astype(F32).astype(BF)
    mine = (iota((BLK // 2, TOK), 0) == group).astype(F32).astype(BF)
    copies[2].wait()
    copies[3].wait()
    rows = jnp.concatenate([act_ref[0], grad_ref[0]], axis=0)
    parts = jnp.concatenate([rows * mine[o : o + 1] for o in range(BLK // 2)], axis=0)
    got = lax.dot_general(parts, hot, NT, preferred_element_type=F32).astype(BF)
    for o in range(BLK // 2):
        send_ref[2 * o] = got[o * W : (o + 1) * W, :LANES]
        send_ref[2 * o + 1] = got[o * W : (o + 1) * W, LANES:]
    for copy in copies[4:]:
        copy.wait()


def split(x):
    hi = x.astype(BF)
    return hi, (x - hi.astype(F32)).astype(BF)


def dot(a, b):
    return jnp.dot(a, b, preferred_element_type=F32)


def cond_kernel(recv_ref, po_ref, pi_ref, cond_ref, square_ref):
    span = OWN // 4
    wide = BLK * span * MOST
    mask = (iota((span * A, wide), 0) // A) == (iota((span * A, wide), 1) // MOST % span)
    docs = []
    for q in range(4):
        cols = slice(q * span * MOST, (q + 1) * span * MOST)
        both = jnp.concatenate([recv_ref[s][:, cols] for s in range(BLK)], axis=1)
        spread = jnp.concatenate([both[:A]] * span, axis=0)
        spread = jnp.where(mask, spread, jnp.zeros_like(spread))
        docs.append(lax.dot_general(both[A:], spread, NT, preferred_element_type=F32))
    doc = jnp.concatenate(docs, axis=1)
    po_hi, po_lo = split(po_ref[0])
    d_hi, d_lo = split(doc)
    left = dot(
        jnp.concatenate([po_hi, po_hi, po_lo, po_lo], axis=1),
        jnp.concatenate([d_hi, d_lo, d_hi, d_lo], axis=0),
    )
    pick = (iota((A, 256), 0) == iota((A, 256), 1) % A).astype(F32).astype(BF)
    diag = (iota((256, 256), 0) // A) == (iota((256, 256), 1) // A)

    def block_diagonal(part):
        row = dot(part, pick)
        full = jnp.concatenate([row] * 8, axis=0)
        return jnp.where(diag, full, 0.0).astype(BF)

    pi_hi, pi_lo = split(pi_ref[0])
    pi_hi, pi_lo = block_diagonal(pi_hi), block_diagonal(pi_lo)
    l_hi, l_lo = split(left)
    def stack(part):
        return jnp.concatenate([part[:, q * 256 : (q + 1) * 256] for q in range(OWN * A // 256)], axis=0)

    l_hi, l_lo = stack(l_hi), stack(l_lo)
    both = dot(jnp.concatenate([l_hi, l_lo], axis=0), pi_hi)
    cond = both[:256] + both[256:] + dot(l_hi, pi_lo)
    cond = jnp.concatenate([cond[q * G : (q + 1) * G] for q in range(OWN * A // 256)], axis=1)
    cond = jnp.transpose(cond.reshape(G, OWN, A), (1, 0, 2)).reshape(OWN, F)
    cond_ref[...] = cond
    square = jnp.sum(cond * cond, axis=1, keepdims=True)
    row = jnp.transpose(jnp.broadcast_to(square, (OWN, 128)))[:8]
    row = jnp.concatenate([row, jnp.zeros((8, 128 - OWN), F32)], axis=1)
    for m in range(BLK):
        square_ref[m] = row


def scale_kernel(cond_ref, squares_ref, doc_ref):
    total = jnp.sum(squares_ref[...], axis=0)
    inverse = 1.0 / jnp.sqrt(total + 1e-6)
    inverse = jnp.transpose(jnp.broadcast_to(inverse[:1], (8, 128)))[:OWN, :1]
    doc_ref[...] = (cond_ref[...] * inverse).astype(BF)


def score_tiles(places, blocks, tiles, out_hbm, buffer, sem):
    x, y, c = (lax.axis_index(a) for a in BLK_AXES)
    docs = jnp.concatenate([b[...] for b in blocks], axis=0)
    copies = []
    for i, tile in enumerate(tiles):
        cols = pl.ds(i * TILE, TILE)
        buffer[:, cols] = lax.dot_general(docs, tile(), NT, preferred_element_type=F32)
        for j, (dx, dy, dc) in enumerate(places):
            at = (((x ^ dx) * 4 + (y + dy) % 4) * 2 + (c ^ dc)) * OWN
            copy = pltpu.make_async_copy(
                buffer.at[pl.ds(j * OWN, OWN), cols],
                out_hbm.at[0, pl.ds(pl.multiple_of(at, OWN), OWN), cols],
                sem.at[i, j],
            )
            copy.start()
            copies.append(copy)
    for copy in copies:
        copy.wait()


def tiles_of(train_ref):
    return [lambda i=i: train_ref[0, i * TILE : (i + 1) * TILE] for i in range(train_ref.shape[1] // TILE)]


def score_kernel(places, count, *refs):
    blocks, train_ref, (out_hbm, buffer, sem) = refs[:count], refs[count], refs[-3:]
    score_tiles(places, blocks, tiles_of(train_ref), out_hbm, buffer, sem)


def swap(x, axis):
    return lax.ppermute(x, axis, [(0, 1), (1, 0)])


def turn(x, by):
    return lax.ppermute(x, "y", [(i, (i + by) % 4) for i in range(4)])


def score(places, blocks, train, *out):
    hbm = pl.BlockSpec(memory_space=pltpu.HBM)
    rows = train.shape[1]
    return pl.pallas_call(
        functools.partial(score_kernel, places, len(blocks)),
        out_shape=pltpu.HBM((1, DOCS, rows), F32),
        in_specs=[VM] * (len(blocks) + 1) + [hbm] * len(out),
        out_specs=hbm,
        scratch_shapes=[
            pltpu.VMEM((len(places) * OWN, rows), F32),
            pltpu.SemaphoreType.DMA((rows // TILE, len(places))),
        ],
        input_output_aliases={len(blocks) + 1: 0} if out else {},
        name="far" if out else "near",
        compiler_params=room(8),
    )(*blocks, train, *out)


def pair(block):
    return [block, swap(block, "core")]


def label(*offsets):
    return [(dx, dy, dc) for dx, dy in offsets for dc in (0, 1)]


def body(act, grad, train, pre_out, pre_in, doc_ids, owners):
    hbm = pl.BlockSpec(memory_space=pltpu.HBM)
    ids, own = doc_ids.reshape(1, TOK), owners.reshape(1, DOCS)
    kept = (pre_out, pre_in, train)
    loaded = (act, grad, ids, own)
    send, pre_out, pre_in, train = pl.pallas_call(
        slot_kernel,
        out_shape=(
            jax.ShapeDtypeStruct((BLK, W, LANES), BF),
            *(pltpu.VMEM(v.shape, v.dtype) for v in kept),
        ),
        in_specs=[hbm] * 7,
        out_specs=[VM] * 4,
        scratch_shapes=[
            *(pltpu.VMEM(v.shape, v.dtype) for v in loaded),
            pltpu.SemaphoreType.DMA((7,)),
        ],
        name="slots",
        compiler_params=room(24),
    )(*(pltpu.with_memory_space_constraint(v, pltpu.HBM) for v in (*loaded, *kept)))
    received = lax.all_to_all(send, BLK_AXES, split_axis=0, concat_axis=0, tiled=True)
    cond, squares = pl.pallas_call(
        cond_kernel,
        out_shape=(
            jax.ShapeDtypeStruct((OWN, F), F32),
            jax.ShapeDtypeStruct((BLK, 8, 128), F32),
        ),
        in_specs=[VM] * 3,
        out_specs=[VM] * 2,
        name="condition",
        compiler_params=room(16),
    )(received, pre_out, pre_in)
    squares = lax.all_to_all(squares, MOD_AXES, split_axis=0, concat_axis=0, tiled=True)
    doc = pl.pallas_call(
        scale_kernel,
        out_shape=jax.ShapeDtypeStruct((OWN, F), BF),
        in_specs=[VM] * 2,
        out_specs=VM,
        name="scale",
        compiler_params=room(2),
    )(cond, squares)
    side, above, below, over = swap(doc, "xl"), turn(doc, 1), turn(doc, -1), turn(doc, 2)
    side_above, side_below, side_over = swap(above, "xl"), turn(side, -1), swap(over, "xl")
    doc, side, above, below, over = lax.optimization_barrier((doc, side, above, below, over))
    near = pair(doc) + pair(side) + pair(above) + pair(below)
    out = score(label((0, 0), (1, 0), (0, 3), (0, 1)), near, train)
    far = pair(over)
    side_above, side_below, side_over, out = lax.optimization_barrier((side_above, side_below, side_over, out))
    far += pair(side_above) + pair(side_below) + pair(side_over)
    return score(label((0, 2), (1, 3), (1, 1), (1, 2)), far, train, out)


def solution(mesh):
    fine = Mesh(mesh.devices.reshape(2, 4, 2, 2, 8), (*BLK_AXES, *MOD_AXES))
    return jax.shard_map(
        body,
        mesh=fine,
        in_specs=(
            P(MOD_AXES, None, BLK_AXES),
            P(MOD_AXES, None, BLK_AXES),
            P(MOD_AXES, BLK_AXES, None),
            P(MOD_AXES, None, None),
            P(MOD_AXES, None, None),
            P(BLK_AXES, None),
            P(),
        ),
        out_specs=P(MOD_AXES, None, BLK_AXES),
        check_vma=False,
    )
```

```python
import functools

import jax
import jax.numpy as jnp
from jax import lax
from jax.experimental import pallas as pl
from jax.experimental.pallas import tpu as pltpu
from jax.sharding import Mesh, PartitionSpec as P

A = 32
G = 64
W = A + G
MOST = 4
BLK = 16
OWN = 32
DOCS = 512
TOK = 1024
LANES = OWN * MOST
F = G * A
TILE = 512
BF = jnp.bfloat16
F32 = jnp.float32
NT = (((1,), (1,)), ((), ()))
BLK_AXES = ("xl", "y", "core")
MOD_AXES = ("xh", "z")
VM = pl.BlockSpec(memory_space=pltpu.VMEM)


def room(mib):
    return pltpu.CompilerParams(vmem_limit_bytes=mib << 20)


def iota(shape, axis):
    return lax.broadcasted_iota(jnp.int32, shape, axis)


def slot_kernel(act_hbm, grad_hbm, ids_hbm, own_hbm, po_hbm, pi_hbm, train_hbm, send_ref, po_ref, pi_ref, train_ref,
                act_ref, grad_ref, ids_ref, own_ref, sem):
    sources = (ids_hbm, own_hbm, act_hbm, grad_hbm, po_hbm, pi_hbm, train_hbm)
    targets = (ids_ref, own_ref, act_ref, grad_ref, po_ref, pi_ref, train_ref)
    copies = [pltpu.make_async_copy(a, b, sem.at[i]) for i, (a, b) in enumerate(zip(sources, targets))]
    for copy in copies:
        copy.start()
    copies[0].wait()
    copies[1].wait()
    ids = ids_ref[...]
    ids_col = jnp.transpose(jnp.broadcast_to(ids, (8, TOK)))[:, :1]
    own_col = jnp.transpose(jnp.broadcast_to(own_ref[...], (8, DOCS)))[:, :1]
    place = jnp.sum(jnp.where(own_col == ids, iota((DOCS, TOK), 0), 0), axis=0, keepdims=True)
    step = 128
    ranks = []
    for j in range(TOK // step):
        mine = ids[:, j * step : (j + 1) * step]
        there = ids_col[j * step : (j + 1) * step]
        same = (there == mine) & (iota((step, step), 0) < iota((step, step), 1))
        count = jnp.sum(same.astype(jnp.int32), axis=0, keepdims=True)
        if j:
            count += jnp.sum((ids_col[: j * step] == mine).astype(jnp.int32), axis=0, keepdims=True)
        ranks.append(count)
    slot = place * MOST + jnp.concatenate(ranks, axis=1)
    group = slot // 256
    inner = slot % 256
    hot = (iota((256, TOK), 0) == inner).astype(F32).astype(BF)
    mine = (iota((BLK // 2, TOK), 0) == group).astype(F32).astype(BF)
    copies[2].wait()
    copies[3].wait()
    rows = jnp.concatenate([act_ref[0], grad_ref[0]], axis=0)
    parts = jnp.concatenate([rows * mine[o : o + 1] for o in range(BLK // 2)], axis=0)
    got = lax.dot_general(parts, hot, NT, preferred_element_type=F32).astype(BF)
    for o in range(BLK // 2):
        send_ref[2 * o] = got[o * W : (o + 1) * W, :LANES]
        send_ref[2 * o + 1] = got[o * W : (o + 1) * W, LANES:]
    for copy in copies[4:]:
        copy.wait()


def split(x):
    hi = x.astype(BF)
    return hi, (x - hi.astype(F32)).astype(BF)


def dot(a, b):
    return jnp.dot(a, b, preferred_element_type=F32)


def cond_kernel(recv_ref, po_ref, pi_ref, cond_ref, square_ref):
    span = OWN // 4
    wide = BLK * span * MOST
    mask = (iota((span * A, wide), 0) // A) == (iota((span * A, wide), 1) // MOST % span)
    docs = []
    for q in range(4):
        cols = slice(q * span * MOST, (q + 1) * span * MOST)
        both = jnp.concatenate([recv_ref[s][:, cols] for s in range(BLK)], axis=1)
        spread = jnp.concatenate([both[:A]] * span, axis=0)
        spread = jnp.where(mask, spread, jnp.zeros_like(spread))
        docs.append(lax.dot_general(both[A:], spread, NT, preferred_element_type=F32))
    doc = jnp.concatenate(docs, axis=1)
    po_hi, po_lo = split(po_ref[0])
    d_hi, d_lo = split(doc)
    left = dot(
        jnp.concatenate([po_hi, po_hi, po_lo, po_lo], axis=1),
        jnp.concatenate([d_hi, d_lo, d_hi, d_lo], axis=0),
    )
    pick = (iota((A, 256), 0) == iota((A, 256), 1) % A).astype(F32).astype(BF)
    diag = (iota((256, 256), 0) // A) == (iota((256, 256), 1) // A)

    def block_diagonal(part):
        row = dot(part, pick)
        full = jnp.concatenate([row] * 8, axis=0)
        return jnp.where(diag, full, 0.0).astype(BF)

    pi_hi, pi_lo = split(pi_ref[0])
    pi_hi, pi_lo = block_diagonal(pi_hi), block_diagonal(pi_lo)
    l_hi, l_lo = split(left)
    def stack(part):
        return jnp.concatenate([part[:, q * 256 : (q + 1) * 256] for q in range(OWN * A // 256)], axis=0)

    l_hi, l_lo = stack(l_hi), stack(l_lo)
    both = dot(jnp.concatenate([l_hi, l_lo], axis=0), pi_hi)
    cond = both[:256] + both[256:] + dot(l_hi, pi_lo)
    cond = jnp.concatenate([cond[q * G : (q + 1) * G] for q in range(OWN * A // 256)], axis=1)
    cond = jnp.transpose(cond.reshape(G, OWN, A), (1, 0, 2)).reshape(OWN, F)
    cond_ref[...] = cond
    square = jnp.sum(cond * cond, axis=1, keepdims=True)
    row = jnp.transpose(jnp.broadcast_to(square, (OWN, 128)))[:8]
    row = jnp.concatenate([row, jnp.zeros((8, 128 - OWN), F32)], axis=1)
    square_ref[...] = jnp.concatenate([row] * (BLK // 8), axis=0)


def scale_kernel(cond_ref, squares_ref, doc_ref):
    total = jnp.sum(squares_ref[...], axis=0, keepdims=True)
    inverse = 1.0 / jnp.sqrt(total + 1e-6)
    inverse = jnp.transpose(jnp.broadcast_to(inverse, (8, 128)))[:OWN, :1]
    doc_ref[...] = (cond_ref[...] * inverse).astype(BF)


def score_tiles(places, blocks, tiles, out_hbm, buffer, sem):
    x, y, c = (lax.axis_index(a) for a in BLK_AXES)
    docs = jnp.concatenate([b[...] for b in blocks], axis=0)
    copies = []
    for i, tile in enumerate(tiles):
        cols = pl.ds(i * TILE, TILE)
        buffer[:, cols] = lax.dot_general(docs, tile(), NT, preferred_element_type=F32)
        for j, (dx, dy, dc) in enumerate(places):
            at = (((x ^ dx) * 4 + (y + dy) % 4) * 2 + (c ^ dc)) * OWN
            copy = pltpu.make_async_copy(
                buffer.at[pl.ds(j * OWN, OWN), cols],
                out_hbm.at[0, pl.ds(pl.multiple_of(at, OWN), OWN), cols],
                sem.at[i, j],
            )
            copy.start()
            copies.append(copy)
    for copy in copies:
        copy.wait()


def tiles_of(train_ref):
    return [lambda i=i: train_ref[0, i * TILE : (i + 1) * TILE] for i in range(train_ref.shape[1] // TILE)]


def score_kernel(places, count, *refs):
    blocks, train_ref, (out_hbm, buffer, sem) = refs[:count], refs[count], refs[-3:]
    score_tiles(places, blocks, tiles_of(train_ref), out_hbm, buffer, sem)


def swap(x, axis):
    return lax.ppermute(x, axis, [(0, 1), (1, 0)])


def turn(x, by):
    return lax.ppermute(x, "y", [(i, (i + by) % 4) for i in range(4)])


def score(places, blocks, train, *out):
    hbm = pl.BlockSpec(memory_space=pltpu.HBM)
    rows = train.shape[1]
    return pl.pallas_call(
        functools.partial(score_kernel, places, len(blocks)),
        out_shape=pltpu.HBM((1, DOCS, rows), F32),
        in_specs=[VM] * (len(blocks) + 1) + [hbm] * len(out),
        out_specs=hbm,
        scratch_shapes=[
            pltpu.VMEM((len(places) * OWN, rows), F32),
            pltpu.SemaphoreType.DMA((rows // TILE, len(places))),
        ],
        input_output_aliases={len(blocks) + 1: 0} if out else {},
        name="far" if out else "near",
        compiler_params=room(8),
    )(*blocks, train, *out)


def pair(block):
    return [block, swap(block, "core")]


def label(*offsets):
    return [(dx, dy, dc) for dx, dy in offsets for dc in (0, 1)]


def body(act, grad, train, pre_out, pre_in, doc_ids, owners):
    hbm = pl.BlockSpec(memory_space=pltpu.HBM)
    ids, own = doc_ids.reshape(1, TOK), owners.reshape(1, DOCS)
    kept = (pre_out, pre_in, train)
    loaded = (act, grad, ids, own)
    send, pre_out, pre_in, train = pl.pallas_call(
        slot_kernel,
        out_shape=(
            jax.ShapeDtypeStruct((BLK, W, LANES), BF),
            *(pltpu.VMEM(v.shape, v.dtype) for v in kept),
        ),
        in_specs=[hbm] * 7,
        out_specs=[VM] * 4,
        scratch_shapes=[
            *(pltpu.VMEM(v.shape, v.dtype) for v in loaded),
            pltpu.SemaphoreType.DMA((7,)),
        ],
        name="slots",
        compiler_params=room(24),
    )(*(pltpu.with_memory_space_constraint(v, pltpu.HBM) for v in (*loaded, *kept)))
    received = lax.all_to_all(send, BLK_AXES, split_axis=0, concat_axis=0, tiled=True)
    cond, squares = pl.pallas_call(
        cond_kernel,
        out_shape=(
            jax.ShapeDtypeStruct((OWN, F), F32),
            jax.ShapeDtypeStruct((BLK, 128), F32),
        ),
        in_specs=[VM] * 3,
        out_specs=[VM] * 2,
        name="condition",
        compiler_params=room(16),
    )(received, pre_out, pre_in)
    squares = lax.all_to_all(squares, MOD_AXES, split_axis=0, concat_axis=0, tiled=True)
    doc = pl.pallas_call(
        scale_kernel,
        out_shape=jax.ShapeDtypeStruct((OWN, F), BF),
        in_specs=[VM] * 2,
        out_specs=VM,
        name="scale",
        compiler_params=room(2),
    )(cond, squares)
    side, above, below, over = swap(doc, "xl"), turn(doc, 1), turn(doc, -1), turn(doc, 2)
    side_above, side_below, side_over = swap(above, "xl"), turn(side, -1), swap(over, "xl")
    side, above, below, over = lax.optimization_barrier((side, above, below, over))
    near = pair(doc) + pair(side) + pair(above) + pair(below)
    out = score(label((0, 0), (1, 0), (0, 3), (0, 1)), near, train)
    far = pair(over)
    side_above, side_below, side_over, out = lax.optimization_barrier((side_above, side_below, side_over, out))
    far += pair(side_above) + pair(side_below) + pair(side_over)
    return score(label((0, 2), (1, 3), (1, 1), (1, 2)), far, train, out)


def solution(mesh):
    fine = Mesh(mesh.devices.reshape(2, 4, 2, 2, 8), (*BLK_AXES, *MOD_AXES))
    return jax.shard_map(
        body,
        mesh=fine,
        in_specs=(
            P(MOD_AXES, None, BLK_AXES),
            P(MOD_AXES, None, BLK_AXES),
            P(MOD_AXES, BLK_AXES, None),
            P(MOD_AXES, None, None),
            P(MOD_AXES, None, None),
            P(BLK_AXES, None),
            P(),
        ),
        out_specs=P(MOD_AXES, None, BLK_AXES),
        check_vma=False,
    )
```

```python
import functools

import jax
import jax.numpy as jnp
from jax import lax
from jax.experimental import pallas as pl
from jax.experimental.pallas import tpu as pltpu
from jax.sharding import Mesh, PartitionSpec as P

A = 32
G = 64
W = A + G
MOST = 4
BLK = 16
OWN = 32
DOCS = 512
TOK = 1024
LANES = OWN * MOST
F = G * A
TILE = 512
REST = 256
BF = jnp.bfloat16
F32 = jnp.float32
NT = (((1,), (1,)), ((), ()))
BLK_AXES = ("xl", "y", "core")
MOD_AXES = ("xh", "z")
VM = pl.BlockSpec(memory_space=pltpu.VMEM)


def room(mib):
    return pltpu.CompilerParams(vmem_limit_bytes=mib << 20)


def iota(shape, axis):
    return lax.broadcasted_iota(jnp.int32, shape, axis)


def slot_kernel(act_hbm, grad_hbm, ids_hbm, own_hbm, po_hbm, pi_hbm, train_hbm, send_ref, po_ref, pi_ref, train_ref,
                act_ref, grad_ref, ids_ref, own_ref, sem):
    sources = (ids_hbm, own_hbm, act_hbm, grad_hbm, po_hbm, pi_hbm, train_hbm.at[:, : train_ref.shape[1]])
    targets = (ids_ref, own_ref, act_ref, grad_ref, po_ref, pi_ref, train_ref)
    copies = [pltpu.make_async_copy(a, b, sem.at[i]) for i, (a, b) in enumerate(zip(sources, targets))]
    for copy in copies:
        copy.start()
    copies[0].wait()
    copies[1].wait()
    ids = ids_ref[...]
    ids_col = jnp.transpose(jnp.broadcast_to(ids, (8, TOK)))[:, :1]
    own_col = jnp.transpose(jnp.broadcast_to(own_ref[...], (8, DOCS)))[:, :1]
    place = jnp.sum(jnp.where(own_col == ids, iota((DOCS, TOK), 0), 0), axis=0, keepdims=True)
    step = 128
    ranks = []
    for j in range(TOK // step):
        mine = ids[:, j * step : (j + 1) * step]
        there = ids_col[j * step : (j + 1) * step]
        same = (there == mine) & (iota((step, step), 0) < iota((step, step), 1))
        count = jnp.sum(same.astype(jnp.int32), axis=0, keepdims=True)
        if j:
            count += jnp.sum((ids_col[: j * step] == mine).astype(jnp.int32), axis=0, keepdims=True)
        ranks.append(count)
    slot = place * MOST + jnp.concatenate(ranks, axis=1)
    group = slot // 256
    inner = slot % 256
    hot = (iota((256, TOK), 0) == inner).astype(F32).astype(BF)
    mine = (iota((BLK // 2, TOK), 0) == group).astype(F32).astype(BF)
    copies[2].wait()
    copies[3].wait()
    rows = jnp.concatenate([act_ref[0], grad_ref[0]], axis=0)
    parts = jnp.concatenate([rows * mine[o : o + 1] for o in range(BLK // 2)], axis=0)
    got = lax.dot_general(parts, hot, NT, preferred_element_type=F32).astype(BF)
    for o in range(BLK // 2):
        send_ref[2 * o] = got[o * W : (o + 1) * W, :LANES]
        send_ref[2 * o + 1] = got[o * W : (o + 1) * W, LANES:]
    for copy in copies[4:]:
        copy.wait()


def split(x):
    hi = x.astype(BF)
    return hi, (x - hi.astype(F32)).astype(BF)


def dot(a, b):
    return jnp.dot(a, b, preferred_element_type=F32)


def cond_kernel(recv_ref, po_ref, pi_ref, train_hbm, cond_ref, square_ref, rest_ref, sem):
    copy = pltpu.make_async_copy(train_hbm.at[:, train_hbm.shape[1] - REST :], rest_ref, sem)
    copy.start()
    span = OWN // 4
    wide = BLK * span * MOST
    mask = (iota((span * A, wide), 0) // A) == (iota((span * A, wide), 1) // MOST % span)
    docs = []
    for q in range(4):
        cols = slice(q * span * MOST, (q + 1) * span * MOST)
        both = jnp.concatenate([recv_ref[s][:, cols] for s in range(BLK)], axis=1)
        spread = jnp.concatenate([both[:A]] * span, axis=0)
        spread = jnp.where(mask, spread, jnp.zeros_like(spread))
        docs.append(lax.dot_general(both[A:], spread, NT, preferred_element_type=F32))
    doc = jnp.concatenate(docs, axis=1)
    po_hi, po_lo = split(po_ref[0])
    d_hi, d_lo = split(doc)
    left = dot(
        jnp.concatenate([po_hi, po_hi, po_lo, po_lo], axis=1),
        jnp.concatenate([d_hi, d_lo, d_hi, d_lo], axis=0),
    )
    pick = (iota((A, 256), 0) == iota((A, 256), 1) % A).astype(F32).astype(BF)
    diag = (iota((256, 256), 0) // A) == (iota((256, 256), 1) // A)

    def block_diagonal(part):
        row = dot(part, pick)
        full = jnp.concatenate([row] * 8, axis=0)
        return jnp.where(diag, full, 0.0).astype(BF)

    pi_hi, pi_lo = split(pi_ref[0])
    pi_hi, pi_lo = block_diagonal(pi_hi), block_diagonal(pi_lo)
    l_hi, l_lo = split(left)
    def stack(part):
        return jnp.concatenate([part[:, q * 256 : (q + 1) * 256] for q in range(OWN * A // 256)], axis=0)

    l_hi, l_lo = stack(l_hi), stack(l_lo)
    both = dot(jnp.concatenate([l_hi, l_lo], axis=0), pi_hi)
    cond = both[:256] + both[256:] + dot(l_hi, pi_lo)
    cond = jnp.concatenate([cond[q * G : (q + 1) * G] for q in range(OWN * A // 256)], axis=1)
    cond = jnp.transpose(cond.reshape(G, OWN, A), (1, 0, 2)).reshape(OWN, F)
    cond_ref[...] = cond
    square = jnp.sum(cond * cond, axis=1, keepdims=True)
    row = jnp.transpose(jnp.broadcast_to(square, (OWN, 128)))[:8]
    row = jnp.concatenate([row, jnp.zeros((8, 128 - OWN), F32)], axis=1)
    square_ref[...] = jnp.concatenate([row] * (BLK // 8), axis=0)
    copy.wait()


def scale_kernel(cond_ref, squares_ref, doc_ref):
    total = jnp.sum(squares_ref[...], axis=0, keepdims=True)
    inverse = 1.0 / jnp.sqrt(total + 1e-6)
    inverse = jnp.transpose(jnp.broadcast_to(inverse, (8, 128)))[:OWN, :1]
    doc_ref[...] = (cond_ref[...] * inverse).astype(BF)


def score_tiles(places, blocks, tiles, out_hbm, buffer, sem):
    x, y, c = (lax.axis_index(a) for a in BLK_AXES)
    docs = jnp.concatenate([b[...] for b in blocks], axis=0)
    copies = []
    for i, tile in enumerate(tiles):
        cols = pl.ds(i * TILE, TILE)
        buffer[:, cols] = lax.dot_general(docs, tile(), NT, preferred_element_type=F32)
        for j, (dx, dy, dc) in enumerate(places):
            at = (((x ^ dx) * 4 + (y + dy) % 4) * 2 + (c ^ dc)) * OWN
            copy = pltpu.make_async_copy(
                buffer.at[pl.ds(j * OWN, OWN), cols],
                out_hbm.at[0, pl.ds(pl.multiple_of(at, OWN), OWN), cols],
                sem.at[i, j],
            )
            copy.start()
            copies.append(copy)
    for copy in copies:
        copy.wait()


def tiles_of(train_ref, rest_ref):
    full = train_ref.shape[1] // TILE
    tiles = [lambda i=i: train_ref[0, i * TILE : (i + 1) * TILE] for i in range(full)]
    return tiles + [lambda: jnp.concatenate([train_ref[0, full * TILE :], rest_ref[0]], axis=0)]


def score_kernel(places, count, *refs):
    blocks, trains, (out_hbm, buffer, sem) = refs[:count], refs[count : count + 2], refs[-3:]
    score_tiles(places, blocks, tiles_of(*trains), out_hbm, buffer, sem)


def swap(x, axis):
    return lax.ppermute(x, axis, [(0, 1), (1, 0)])


def turn(x, by):
    return lax.ppermute(x, "y", [(i, (i + by) % 4) for i in range(4)])


def score(places, blocks, train, *out):
    hbm = pl.BlockSpec(memory_space=pltpu.HBM)
    rows = sum(t.shape[1] for t in train)
    return pl.pallas_call(
        functools.partial(score_kernel, places, len(blocks)),
        out_shape=pltpu.HBM((1, DOCS, rows), F32),
        in_specs=[VM] * (len(blocks) + 2) + [hbm] * len(out),
        out_specs=hbm,
        scratch_shapes=[
            pltpu.VMEM((len(places) * OWN, rows), F32),
            pltpu.SemaphoreType.DMA((rows // TILE, len(places))),
        ],
        input_output_aliases={len(blocks) + 2: 0} if out else {},
        name="far" if out else "near",
        compiler_params=room(8),
    )(*blocks, *train, *out)


def pair(block):
    return [block, swap(block, "core")]


def label(*offsets):
    return [(dx, dy, dc) for dx, dy in offsets for dc in (0, 1)]


def body(act, grad, train, pre_out, pre_in, doc_ids, owners):
    hbm = pl.BlockSpec(memory_space=pltpu.HBM)
    ids, own = doc_ids.reshape(1, TOK), owners.reshape(1, DOCS)
    train = pltpu.with_memory_space_constraint(train, pltpu.HBM)
    kept = (pre_out, pre_in, train)
    loaded = (act, grad, ids, own)
    send, pre_out, pre_in, first = pl.pallas_call(
        slot_kernel,
        out_shape=(
            jax.ShapeDtypeStruct((BLK, W, LANES), BF),
            *(pltpu.VMEM(v.shape, v.dtype) for v in kept[:2]),
            pltpu.VMEM((1, train.shape[1] - REST, F), BF),
        ),
        in_specs=[hbm] * 7,
        out_specs=[VM] * 4,
        scratch_shapes=[
            *(pltpu.VMEM(v.shape, v.dtype) for v in loaded),
            pltpu.SemaphoreType.DMA((7,)),
        ],
        name="slots",
        compiler_params=room(24),
    )(*(pltpu.with_memory_space_constraint(v, pltpu.HBM) for v in (*loaded, *kept[:2])), train)
    received = lax.all_to_all(send, BLK_AXES, split_axis=0, concat_axis=0, tiled=True)
    cond, squares, rest = pl.pallas_call(
        cond_kernel,
        out_shape=(
            jax.ShapeDtypeStruct((OWN, F), F32),
            jax.ShapeDtypeStruct((BLK, 128), F32),
            pltpu.VMEM((1, REST, F), BF),
        ),
        in_specs=[VM] * 3 + [hbm],
        out_specs=[VM] * 3,
        scratch_shapes=[pltpu.SemaphoreType.DMA],
        name="condition",
        compiler_params=room(16),
    )(received, pre_out, pre_in, train)
    squares = lax.all_to_all(squares, MOD_AXES, split_axis=0, concat_axis=0, tiled=True)
    doc = pl.pallas_call(
        scale_kernel,
        out_shape=jax.ShapeDtypeStruct((OWN, F), BF),
        in_specs=[VM] * 2,
        out_specs=VM,
        name="scale",
        compiler_params=room(2),
    )(cond, squares)
    train = (first, rest)
    side, above, below, over = swap(doc, "xl"), turn(doc, 1), turn(doc, -1), turn(doc, 2)
    side_above, side_below, side_over = swap(above, "xl"), turn(side, -1), swap(over, "xl")
    side, above, below, over = lax.optimization_barrier((side, above, below, over))
    near = pair(doc) + pair(side) + pair(above) + pair(below)
    out = score(label((0, 0), (1, 0), (0, 3), (0, 1)), near, train)
    far = pair(over)
    side_above, side_below, side_over, out = lax.optimization_barrier((side_above, side_below, side_over, out))
    far += pair(side_above) + pair(side_below) + pair(side_over)
    return score(label((0, 2), (1, 3), (1, 1), (1, 2)), far, train, out)


def solution(mesh):
    fine = Mesh(mesh.devices.reshape(2, 4, 2, 2, 8), (*BLK_AXES, *MOD_AXES))
    return jax.shard_map(
        body,
        mesh=fine,
        in_specs=(
            P(MOD_AXES, None, BLK_AXES),
            P(MOD_AXES, None, BLK_AXES),
            P(MOD_AXES, BLK_AXES, None),
            P(MOD_AXES, None, None),
            P(MOD_AXES, None, None),
            P(BLK_AXES, None),
            P(),
        ),
        out_specs=P(MOD_AXES, None, BLK_AXES),
        check_vma=False,
    )
```
